32 devices in a mesh: seq: 8 (over y, x, core), head: 4 (over z).
Axes of the slice: x: 2, y: 2, z: 4, core: 2. Of those that a mesh axis runs over, the one named last changes fastest.
Arguments:
- hidden: bfloat16 [2, 4096, 1536], P(None, 'seq', 'head'), may hold values from -6 to 6
- norm_gain: float32 [1536], replicated, may hold values from 0.5 to 1.5
- gate_proj: bfloat16 [1536, 3072], P(None, 'head'), may hold values from -0.15625 to 0.15625
- value_proj: bfloat16 [1536, 3072], P(None, 'head'), may hold values from -0.15625 to 0.15625
- state_proj: bfloat16 [1536, 256], replicated, may hold values from -0.15625 to 0.15625
- step_proj: bfloat16 [1536, 48], P(None, 'head'), may hold values from -0.15625 to 0.15625
- conv_value: float32 [4, 3072], P(None, 'head'), may hold values from -3 to 3
- conv_value_bias: float32 [3072], P('head'), may hold values from -2 to 2
- conv_state: float32 [4, 256], replicated, may hold values from -3 to 3
- conv_state_bias: float32 [256], replicated, may hold values from -2 to 2
- step_bias: float32 [48], P('head'), may hold values from -4 to -1
- decay_log: float32 [48], P('head'), may hold values from -11 to 1
- skip_gain: float32 [48], P('head'), may hold values from 0.5 to 2
- gate_gain: float32 [3072], P('head'), may hold values from 0.5 to 1.5
- out_proj: bfloat16 [3072, 1536], P('head'), may hold values from -0.109375 to 0.109375
- cotangent: bfloat16 [2, 4096, 1536], P(None, 'seq', 'head'), may hold values from -6 to 6
Outputs:
- block_out: bfloat16 [2, 4096, 1536], P(None, 'seq', 'head')
- hidden_grad: bfloat16 [2, 4096, 1536], P(None, 'seq', 'head')
- norm_gain_grad: float32 [1536], P('head')
- gate_proj_grad: float32 [1536, 3072], P(None, 'head')
- value_proj_grad: float32 [1536, 3072], P(None, 'head')
- state_proj_grad: float32 [1536, 256], replicated
- step_proj_grad: float32 [1536, 48], P(None, 'head')
- conv_value_grad: float32 [4, 3072], P(None, 'head')
- conv_value_bias_grad: float32 [3072], P('head')
- conv_state_grad: float32 [4, 256], replicated
- conv_state_bias_grad: float32 [256], replicated
- step_bias_grad: float32 [48], P('head')
- decay_log_grad: float32 [48], P('head')
- skip_gain_grad: float32 [48], P('head')
- gate_gain_grad: float32 [3072], P('head')
- out_proj_grad: float32 [3072, 1536], P('head')
The draws below stay inside these ranges and needn't reach their ends.
All inputs are finite; a program needn't handle non-finite values.
Results may differ from the reference program's by a relative error of at most 0.025.
The reference program's roundings to bfloat16 on the way count: a program that leaves them out, or rounds other values in their place, can miss the bound.
Values may be sent and summed in bfloat16 or wider, within the bound.
No kernel may reach another device: no remote copies, remote signals or barrier semaphores. Data moves between devices by JAX's collectives and lax.ppermute only.
A program may use at most 192 MiB of HBM per device.

```python
from functools import partial
import jax
import jax.numpy as jnp
from jax import lax

D = 1536
HEADS = 48
HEAD_DIM = 64
STATE = 128
CONV = 4
BLOCK = 256
BATCH = 2
INNER = 3072
LENGTH = 4096


def block_scale(rng, dims, pieces, smallest, largest):
    factor_of, own = 1.0, jax.random.fold_in(rng, 6)
    for dim, blocks in pieces:
        heights = jnp.exp(jax.random.uniform(jax.random.fold_in(own, dim), (blocks,), jnp.float32, smallest / len(pieces), largest / len(pieces)))
        factor_of = factor_of * jnp.repeat(heights, dims[dim] // blocks).reshape([-1 if axis == dim else 1 for axis in range(len(dims))])
    return factor_of


def bell_draw(stream_key, dims, scale, most, pieces=(), kind=jnp.bfloat16):
    drawn = scale * jax.random.normal(stream_key, dims, jnp.float32)
    if pieces:
        drawn = drawn * block_scale(stream_key, dims, pieces, -0.22, 0.18)
    return jnp.clip(drawn, -most, most).astype(kind)


def setup_inputs(seed: int = 0) -> dict:
    key_of = jax.random.split(jax.random.key(seed), 17)
    return {
        "hidden": bell_draw(key_of[0], (BATCH, LENGTH, D), 1.0, 6.0, ((1, 8), (2, 4))),
        "norm_gain": jnp.clip(1.0 + 0.1 * jax.random.normal(key_of[1], (D,), jnp.float32), 0.5, 1.5),
        "gate_proj": bell_draw(key_of[2], (D, INNER), D ** -0.5, 0.15625, ((1, 4),)),
        "value_proj": bell_draw(key_of[3], (D, INNER), D ** -0.5, 0.15625, ((1, 4),)),
        "state_proj": bell_draw(key_of[4], (D, 2 * STATE), D ** -0.5, 0.15625),
        "step_proj": bell_draw(key_of[5], (D, HEADS), D ** -0.5, 0.15625, ((1, 4),)),
        "conv_value": bell_draw(key_of[6], (CONV, INNER), CONV ** -0.5, 3.0, ((1, 4),), jnp.float32),
        "conv_value_bias": bell_draw(key_of[7], (INNER,), 0.3, 2.0, ((0, 4),), jnp.float32),
        "conv_state": bell_draw(key_of[8], (CONV, 2 * STATE), CONV ** -0.5, 3.0, (), jnp.float32),
        "conv_state_bias": bell_draw(key_of[9], (2 * STATE,), 0.3, 2.0, (), jnp.float32),
        "step_bias": jnp.clip(-4.0 + 3.0 * jax.random.uniform(key_of[10], (HEADS,), jnp.float32) ** block_scale(key_of[10], (HEADS,), ((0, 4),), -0.2, 0.2), -4.0, -1.0),
        "decay_log": jnp.clip(-11.0 + 12.0 * jax.random.uniform(key_of[11], (HEADS,), jnp.float32) ** block_scale(key_of[11], (HEADS,), ((0, 4),), -0.2, 0.2), -11.0, 1.0),
        "skip_gain": jnp.clip(0.5 + 1.5 * jax.random.uniform(key_of[12], (HEADS,), jnp.float32) ** block_scale(key_of[12], (HEADS,), ((0, 4),), -0.2, 0.2), 0.5, 2.0),
        "gate_gain": jnp.clip(1.0 + 0.1 * jax.random.normal(key_of[13], (INNER,), jnp.float32), 0.5, 1.5),
        "out_proj": bell_draw(key_of[14], (INNER, D), INNER ** -0.5, 0.109375, ((0, 4),)),
        "cotangent": bell_draw(key_of[15], (BATCH, LENGTH, D), 1.0, 6.0, ((1, 8), (2, 4))),
    }


EPS = 1e-05
HIGH = lax.Precision.HIGHEST

@jax.custom_vjp
def low(v):
    return lax.optimization_barrier(v.astype(jnp.bfloat16)).astype(jnp.float32)

@jax.custom_vjp
def low_back(v):
    return v

def low_keep(v):
    return (low(v), None)

def low_pass(kept, grad):
    return (grad,)

def back_keep(v):
    return (v, None)

def back_low(kept, grad):
    return (low(grad),)
low.defvjp(low_keep, low_pass)
low_back.defvjp(back_keep, back_low)

def matmul(left, right):
    return jnp.dot(left, right, precision=HIGH)

def block_step(skip_gain, carry_state, inputs):
    x_block, b_block, c_block, cum_block, step_block = inputs
    q_len = x_block.shape[0]
    head_count = x_block.shape[1]
    scores = matmul(c_block, b_block.T)
    per_head = low_back(jnp.broadcast_to(scores[None], (head_count, q_len, q_len)))
    cum_heads = cum_block.T
    causal_mask = jnp.tril(jnp.ones((q_len, q_len), dtype=bool))
    spread = cum_heads[:, :, None] - cum_heads[:, None, :]
    damping = jnp.where(causal_mask, jnp.exp(jnp.where(causal_mask, spread, 0.0)), 0.0)
    mixing = low(per_head * damping * step_block.T[:, None, :])
    inside = jnp.einsum('hts,shp->thp', mixing, x_block, precision=HIGH)
    c_scaled = low(jnp.exp(cum_block)[:, :, None] * c_block[:, None, :])
    carried = jnp.einsum('thn,hpn->thp', c_scaled, low(carry_state), precision=HIGH)
    output = low_back(inside + carried + skip_gain[None, :, None] * x_block)
    block_total = cum_block[-1]
    weights = jnp.exp(block_total[None, :] - cum_block) * step_block
    x_weighted = low(x_block * weights[:, :, None])
    local_state = low_back(jnp.einsum('shp,sn->hpn', x_weighted, b_block, precision=HIGH))
    return (jnp.exp(block_total)[:, None, None] * carry_state + local_state, output)

def layer(weights, sequence):
    norm_gain, gate_proj, value_proj, state_proj, step_proj, conv_value, conv_value_bias, conv_state, conv_state_bias, step_bias, decay_log, skip_gain, gate_gain, out_proj = weights
    length = sequence.shape[0]
    inv_rms = lax.rsqrt(lax.optimization_barrier(jnp.mean(sequence * sequence, -1, keepdims=True)) + EPS)
    normed = low(sequence * inv_rms * norm_gain)
    gate_in = low_back(matmul(normed, gate_proj))
    conv_in = low_back(matmul(normed, jnp.concatenate([value_proj, state_proj], 1)))
    step_raw = low_back(matmul(normed, step_proj))
    kernel = jnp.concatenate([conv_value, conv_state], 1)
    kernel_bias = jnp.concatenate([conv_value_bias, conv_state_bias])
    padded = jnp.pad(conv_in, ((CONV - 1, 0), (0, 0)))
    mixed = kernel_bias + sum((kernel[offset] * padded[offset:offset + length] for offset in range(CONV)))
    activated = jax.nn.silu(mixed)
    blocks = length // BLOCK
    x_values = low(activated[:, :INNER]).reshape(blocks, BLOCK, HEADS, HEAD_DIM)
    b_values = low(activated[:, INNER:INNER + STATE]).reshape(blocks, BLOCK, STATE)
    c_values = low(activated[:, INNER + STATE:]).reshape(blocks, BLOCK, STATE)
    step_size = jax.nn.softplus(step_raw + step_bias)
    log_decay = -jnp.exp(decay_log) * step_size
    cumulative = jnp.cumsum(log_decay.reshape(blocks, BLOCK, HEADS), axis=1)
    start_state = jnp.zeros((HEADS, HEAD_DIM, STATE), jnp.float32)
    _, outputs = lax.scan(jax.checkpoint(partial(block_step, skip_gain)), start_state, (x_values, b_values, c_values, cumulative, step_size.reshape(blocks, BLOCK, HEADS)))
    ssd_out = outputs.reshape(length, INNER)
    gated = ssd_out * jax.nn.silu(gate_in)
    inv_gate = lax.rsqrt(lax.optimization_barrier(jnp.mean(gated * gated, -1, keepdims=True)) + EPS)
    normal_gated = low(gated * inv_gate * gate_gain)
    return sequence + matmul(normal_gated, out_proj)

def reference(hidden, norm_gain, gate_proj, value_proj, state_proj, step_proj, conv_value, conv_value_bias, conv_state, conv_state_bias, step_bias, decay_log, skip_gain, gate_gain, out_proj, cotangent):
    params = tuple((weight_in.astype(jnp.float32) for weight_in in (norm_gain, gate_proj, value_proj, state_proj, step_proj, conv_value, conv_value_bias, conv_state, conv_state_bias, step_bias, decay_log, skip_gain, gate_gain, out_proj)))

    def forward(source, *weights):

        def single(sequence):
            return layer(weights, sequence)
        return lax.map(jax.checkpoint(single), source)
    result, pullback = jax.vjp(forward, hidden.astype(jnp.float32), *params)
    gradients = pullback(cotangent.astype(jnp.float32))
    return (result.astype(jnp.bfloat16), gradients[0].astype(jnp.bfloat16), gradients[1], gradients[2], gradients[3], gradients[4], gradients[5], gradients[6], gradients[7], gradients[8], gradients[9], gradients[10], gradients[11], gradients[12], gradients[13], gradients[14])
```

```python
from functools import partial

import jax
import jax.numpy as jnp
from jax import lax
from jax.experimental import pallas as pl
from jax.experimental.pallas import tpu as pltpu
from jax.sharding import PartitionSpec as P

HEAD_DIM = 64
STATE = 128
CONV = 4
BLOCK = 256
EPS = 1e-05
EDGE = 8
PAD = 16

bf16 = jnp.bfloat16
f32 = jnp.float32

NN = (((1,), (0,)), ((), ()))
NT = (((1,), (1,)), ((), ()))
TN = (((0,), (0,)), ((), ()))


def dot(left, right, dims=NN):
    return lax.dot_general(left, right, dims, preferred_element_type=f32)


def parts_of(value, count):
    parts, rest = [], value
    for _ in range(count - 1):
        part = rest.astype(bf16)
        parts.append(part)
        rest = rest - part.astype(f32)
    parts.append(rest.astype(bf16))
    return parts


def head_map(heads, width):
    head = lax.broadcasted_iota(jnp.int32, (heads, width), 0)
    channel = lax.broadcasted_iota(jnp.int32, (heads, width), 1)
    return ((channel >> 6) == head).astype(bf16)


def spread(value, hmap, count=2):
    return sum(dot(part, hmap) for part in parts_of(value, count))


def per_head(value, hmap, count=2):
    return sum(dot(part, hmap, NT) for part in parts_of(value, count))


def triangle(lower):
    row = lax.broadcasted_iota(jnp.int32, (BLOCK, BLOCK), 0)
    col = lax.broadcasted_iota(jnp.int32, (BLOCK, BLOCK), 1)
    return (row >= col) if lower else (row <= col)


def running_sum(value, lower):
    tri = jnp.where(triangle(lower), 1.0, 0.0).astype(bf16)
    return sum(dot(tri, part) for part in parts_of(value, 3))


def sigmoid(value):
    return 1.0 / (1.0 + jnp.exp(-value))


def softplus(value):
    return jnp.maximum(value, 0.0) + jnp.log1p(jnp.exp(-jnp.abs(value)))


def silu_slope(value):
    sigma = sigmoid(value)
    return sigma * (1.0 + value * (1.0 - sigma))


def shifted_taps(source, taps, start, rows):
    return sum(taps[k : k + 1, :] * source[pl.ds(start + k, rows), :] for k in range(CONV))


def pack_state(out, state, decay):
    out[0, :STATE, :] = state.astype(bf16)
    high = decay.astype(bf16)
    rest = (decay - high.astype(f32)).astype(bf16)
    row = lax.broadcasted_iota(jnp.int32, (PAD, state.shape[1]), 0)
    tail = jnp.where(row == 0, high.astype(f32), jnp.where(row == 1, rest.astype(f32), 0.0))
    out[0, STATE:, :] = tail.astype(bf16)


def project_kernel(
    rows, edge, gain, gate_w, value_w, state_w, step_w, tap_v, bias_v, tap_s, bias_s, step_bias, decay_log,
    normed_o, inv_o, gate_o, cv_o, cs_o, mv_o, ms_o, x_o, b_o, c_o, raw_o, step_o, cum_o, cumt_o, stept_o,
    local_o, pack_o, ev_o, es_o,
    ext_v, ext_s, held, factor,
):
    j, last = pl.program_id(1), pl.num_programs(1) - 1
    heads, width = step_w.shape[1], value_w.shape[1]
    hmap = head_map(heads, width)

    def norm(block):
        block = block.astype(f32)
        inv = lax.rsqrt(jnp.mean(block * block, -1, keepdims=True) + EPS)
        return (block * inv * gain[...]).astype(bf16), inv

    @pl.when(j == 0)
    def _():
        before, _ = norm(edge[0])
        edge_v = dot(before, value_w[...])[PAD - EDGE :]
        edge_s = dot(before, state_w[...])[PAD - EDGE :]
        ext_v[:EDGE, :] = edge_v
        ext_s[:EDGE, :] = edge_s
        ev_o[0] = edge_v
        es_o[0] = edge_s
        held[...] = jnp.zeros_like(held)
        factor[...] = jnp.ones_like(factor)

    @pl.when(j > 0)
    def _():
        ext_v[:EDGE, :] = ext_v[BLOCK:, :]
        ext_s[:EDGE, :] = ext_s[BLOCK:, :]

    normed, inv = norm(rows[...])
    normed_o[...] = normed
    inv_o[...] = jnp.broadcast_to(inv, inv_o.shape)
    gate_o[...] = dot(normed, gate_w[...])
    conv_v = dot(normed, value_w[...])
    conv_s = dot(normed, state_w[...])
    raw = dot(normed, step_w[...])
    cv_o[...] = conv_v
    cs_o[...] = conv_s
    ext_v[EDGE:, :] = conv_v
    ext_s[EDGE:, :] = conv_s
    mixed_v = bias_v[...] + shifted_taps(ext_v, tap_v, EDGE - CONV + 1, BLOCK)
    mixed_s = bias_s[...] + shifted_taps(ext_s, tap_s, EDGE - CONV + 1, BLOCK)
    mv_o[...] = mixed_v
    ms_o[...] = mixed_s
    x = (mixed_v * sigmoid(mixed_v)).astype(bf16)
    maps = (mixed_s * sigmoid(mixed_s)).astype(bf16)
    x_o[...] = x
    b_o[...] = maps[:, :STATE]
    c_o[...] = maps[:, STATE:]

    step = softplus(raw + step_bias[...])
    cum = running_sum(-jnp.exp(decay_log[...]) * step, True)
    raw_o[...] = raw
    step_o[...] = step
    cum_o[...] = cum
    cumt_o[0] = cum.T
    stept_o[0] = step.T
    total = cum[BLOCK - 1 :]
    weights = jnp.exp(total - cum) * step
    x_weighted = (x.astype(f32) * spread(weights, hmap)).astype(bf16)
    local = dot(maps[:, :STATE], x_weighted, TN)
    local_o[0] = local
    decay = spread(jnp.exp(cum[BLOCK - 8 :]), hmap)[7:]
    held[...] = decay * held[...] + local
    factor[...] = decay * factor[...]

    @pl.when(j == last)
    def _():
        pack_state(pack_o, held[...], factor[...])


def within_kernel(x, b, c, cum, cumt, stept, skip, y_o):
    heads, width = cum.shape[1], x.shape[1]
    hmap = head_map(heads, width)
    causal = triangle(True)
    scores = dot(c[...], b[...], NT)
    left = lax.broadcasted_iota(jnp.int32, (BLOCK, 2 * HEAD_DIM), 1) < HEAD_DIM
    for pair in range(heads // 2):
        lanes = slice(pair * 2 * HEAD_DIM, (pair + 1) * 2 * HEAD_DIM)
        x_pair = x[:, lanes]
        inside = []
        for h in (2 * pair, 2 * pair + 1):
            spread_h = jnp.where(causal, cum[:, h : h + 1] - cumt[0, h : h + 1, :], -1e30)
            mixing = (scores * jnp.exp(spread_h) * stept[0, h : h + 1, :]).astype(bf16)
            inside.append(dot(mixing, x_pair))
        y_o[:, lanes] = jnp.where(left, inside[0], inside[1]) + skip[:, lanes] * x_pair.astype(f32)


def output_kernel(
    y, c, cum, local, entering, gate, cot, out_w, gate_gain, ssd_o, grad_o, starts_o, stats_o, state
):
    j = pl.program_id(1)
    heads, width = cum.shape[1], gate.shape[1]
    hmap = head_map(heads, width)

    @pl.when(j == 0)
    def _():
        state[...] = entering[0]

    start = state[...]
    starts_o[0] = start
    scale = spread(jnp.exp(cum[...]), hmap)
    ssd = y[...] + scale * dot(c[...], start.astype(bf16))
    state[...] = scale[BLOCK - 1 :] * start + local[0]
    ssd_o[...] = ssd
    gate_in = gate[...]
    gated = ssd * (gate_in * sigmoid(gate_in))
    grad = dot(cot[...], out_w[...], NT)
    grad_o[...] = grad
    ones = jnp.ones((8, width), bf16)

    def row_sum(value):
        return sum(dot(ones, part, NT) for part in parts_of(value, 3))

    first = lax.broadcasted_iota(jnp.int32, (8, BLOCK), 0) == 0
    stats_o[...] = jnp.where(first, row_sum(gated * gated), row_sum(grad * gate_gain[...] * gated))


def gate_kernel(
    inner, ssd, gate, grad, stats, gate_gain, skip, x, c, cum,
    normal_o, gssd_o, ggate_o, row_o, sgrad_o, sums_o, pack_o, held, factor,
):
    i, j, last = pl.program_id(0), pl.program_id(1), pl.num_programs(1) - 1
    heads, width = cum.shape[1], gate.shape[1]
    hmap = head_map(heads, width)

    @pl.when((i == 0) & (j == 0))
    def _():
        sums_o[...] = jnp.zeros_like(sums_o)

    @pl.when(j == 0)
    def _():
        held[...] = jnp.zeros_like(held)
        factor[...] = jnp.ones_like(factor)

    columns = stats[...].T
    inv_gate = lax.rsqrt(columns[:, 0:1] / inner + EPS)
    mean_dot = inv_gate * columns[:, 1:2] / inner
    gate_in, ssd_out = gate[...], ssd[...]
    sigma = sigmoid(gate_in)
    act = gate_in * sigma
    unit = ssd_out * act * inv_gate
    normal_o[...] = (unit * gate_gain[...]).astype(bf16)
    grad_normal = grad[...]
    grad_gated = inv_gate * (grad_normal * gate_gain[...] - unit * mean_dot)
    grad_ssd = (grad_gated * act).astype(bf16)
    gssd_o[...] = grad_ssd
    ggate_o[...] = (grad_gated * ssd_out * (sigma * (1.0 + gate_in * (1.0 - sigma)))).astype(bf16)
    grad_float, x_float = grad_ssd.astype(f32), x[...].astype(f32)
    row_o[...] = per_head(grad_float * (ssd_out - skip[...] * x_float), hmap)
    gain_sum = jnp.sum(grad_normal * unit, 0, keepdims=True)
    skip_sum = jnp.sum(grad_float * x_float, 0, keepdims=True)
    row = lax.broadcasted_iota(jnp.int32, (8, width), 0)
    sums_o[...] += jnp.where(row == 0, gain_sum, jnp.where(row == 1, skip_sum, 0.0))
    scale = spread(jnp.exp(cum[...]), hmap)
    scaled = (grad_float * scale).astype(bf16)
    state_grad = dot(c[...], scaled, TN)
    sgrad_o[0] = state_grad
    held[...] += factor[...] * state_grad
    factor[...] = factor[...] * scale[BLOCK - 1 :]

    @pl.when(j == last)
    def _():
        pack_state(pack_o, held[...], factor[...])


def score_kernel(x, b, c, cum, cumt, step, gssd, gx_o, gb_o, gc_o, total):
    heads = cum.shape[1]
    causal = triangle(False)
    scores = dot(b[...], c[...], NT)
    left = lax.broadcasted_iota(jnp.int32, (BLOCK, 2 * HEAD_DIM), 1) < HEAD_DIM
    zero = jnp.zeros((BLOCK, 2 * HEAD_DIM), bf16)
    for pair in range(heads // 2):
        lanes = slice(pair * 2 * HEAD_DIM, (pair + 1) * 2 * HEAD_DIM)
        x_pair, g_pair = x[:, lanes], gssd[:, lanes]
        inside = []
        for side in range(2):
            h = 2 * pair + side
            spread_h = jnp.where(causal, cumt[0, h : h + 1, :] - cum[:, h : h + 1], -1e30)
            damping = jnp.exp(spread_h) * step[:, h : h + 1]
            x_head = jnp.where(left, x_pair, zero) if side == 0 else jnp.where(left, zero, x_pair)
            low = (dot(x_head, g_pair, NT) * damping).astype(bf16).astype(f32)
            if h == 0:
                total[...] = low
            else:
                total[...] += low
            inside.append(dot((scores * damping).astype(bf16), g_pair))
        gx_o[:, lanes] = jnp.where(left, inside[0], inside[1])
    high, rest = parts_of(total[...], 2)
    gb_o[...] = dot(high, c[...]) + dot(rest, c[...])
    gc_o[...] = dot(high, b[...], TN) + dot(rest, b[...], TN)


def back_kernel(
    leaving, starts, sgrad, gx_in, gb_in, gc_in, row_term, x, gssd, b, c, raw, step, cum,
    mv, ms, cv, cs, ev, es, tap_v, tap_s, skip, step_bias, decay_log,
    gv_o, gs_o, tailv_o, tails_o, retv_o, rets_o, graw_o, sumv_o, sums_o, sumh_o,
    end, ext_v, ext_s, pre_v, pre_s,
):
    i, j, last = pl.program_id(0), pl.program_id(1), pl.num_programs(1) - 1
    heads, width = cum.shape[1], x.shape[1]
    hmap = head_map(heads, width)

    @pl.when((i == 0) & (j == 0))
    def _():
        sumv_o[...] = jnp.zeros_like(sumv_o)
        sums_o[...] = jnp.zeros_like(sums_o)
        sumh_o[...] = jnp.zeros_like(sumh_o)

    @pl.when(j == 0)
    def _():
        end[...] = leaving[0]
        ext_v[BLOCK:, :] = jnp.zeros((EDGE, ext_v.shape[1]), f32)
        ext_s[BLOCK:, :] = jnp.zeros((EDGE, ext_s.shape[1]), f32)

    @pl.when(j > 0)
    def _():
        ext_v[BLOCK:, :] = ext_v[:EDGE, :]
        ext_s[BLOCK:, :] = ext_s[:EDGE, :]

    end_grad = end[...]
    end_low = end_grad.astype(bf16)
    start = starts[0]
    cum_v, step_v = cum[...], step[...]
    x_float, g_float = x[...].astype(f32), gssd[...].astype(f32)
    remain = jnp.exp(cum_v[BLOCK - 1 :] - cum_v)
    weight = spread(remain * step_v, hmap)
    scale = spread(jnp.exp(cum_v), hmap)
    decay = scale[BLOCK - 1 :]
    grad_weighted = weight * dot(b[...], end_low)
    q_weight = per_head(x_float * grad_weighted, hmap)
    q_mixing = per_head(x_float * gx_in[...], hmap)
    grad_x = gx_in[...] + grad_weighted + skip[...] * g_float
    x_weighted = (x_float * weight).astype(bf16)
    grad_b = gb_in[...] + dot(x_weighted, end_low, NT)
    grad_c = gc_in[...] + dot((g_float * scale).astype(bf16), start.astype(bf16), NT)
    along = jnp.sum(end_grad * start, 0, keepdims=True) * decay
    grad_total = per_head(jnp.broadcast_to(along, (8, width)), hmap)[:1] + jnp.sum(q_weight, 0, keepdims=True)
    end[...] = decay * end_grad + sgrad[0]

    final = lax.broadcasted_iota(jnp.int32, (BLOCK, heads), 0) == BLOCK - 1
    grad_cum = row_term[...] - q_mixing - q_weight + jnp.where(final, grad_total, 0.0)
    grad_log = running_sum(grad_cum, False)
    rate = -jnp.exp(decay_log[...])
    shifted = raw[...] + step_bias[...]
    sigma = sigmoid(shifted)
    ratio = jnp.where(step_v > 0.0, sigma / jnp.where(step_v > 0.0, step_v, 1.0), 1.0)
    grad_raw = grad_log * rate * sigma + (q_mixing + q_weight) * ratio
    graw_o[...] = grad_raw.astype(bf16)
    bias_sum = jnp.sum(grad_raw, 0, keepdims=True)
    decay_sum = jnp.sum(grad_log * rate * step_v, 0, keepdims=True)
    row = lax.broadcasted_iota(jnp.int32, (8, heads), 0)
    sumh_o[...] += jnp.where(row == 0, bias_sum, jnp.where(row == 1, decay_sum, 0.0))

    ext_v[:BLOCK, :] = grad_x * silu_slope(mv[...])
    slope = silu_slope(ms[...])
    ext_s[:BLOCK, :STATE] = grad_b * slope[:, :STATE]
    ext_s[:BLOCK, STATE:] = grad_c * slope[:, STATE:]

    def back(ext, taps, conv, grad_o, tail_o, sum_o):
        grad = sum(taps[k : k + 1, :] * ext[pl.ds(CONV - 1 - k, BLOCK), :] for k in range(CONV))
        grad_o[...] = grad.astype(bf16)

        @pl.when(j == 0)
        def _():
            tail_o[0] = grad[BLOCK - PAD :]

        source = conv[...]
        lines = [
            jnp.sum(source * ext[pl.ds(CONV - 1 - k, BLOCK), :], 0, keepdims=True) for k in range(CONV)
        ]
        lines.append(jnp.sum(ext[:BLOCK, :], 0, keepdims=True))
        place = lax.broadcasted_iota(jnp.int32, sum_o.shape, 0)
        sum_o[...] += sum(jnp.where(place == k, line, 0.0) for k, line in enumerate(lines))

    back(ext_v, tap_v, cv, gv_o, tailv_o, sumv_o)
    back(ext_s, tap_s, cs, gs_o, tails_o, sums_o)

    def before(ext, pre, taps, edge, ret_o, sum_o):
        pre[:EDGE, :] = jnp.zeros((EDGE, pre.shape[1]), f32)
        pre[EDGE:, :] = ext[:EDGE, :]
        views = [pre[pl.ds(CONV - 1 - k, EDGE), :] for k in range(CONV)]
        ret_o[0] = sum(taps[k : k + 1, :] * views[k] for k in range(CONV))
        source = edge[0]
        place = lax.broadcasted_iota(jnp.int32, sum_o.shape, 0)
        sum_o[...] += sum(
            jnp.where(place == k, jnp.sum(source * views[k], 0, keepdims=True), 0.0) for k in range(CONV)
        )

    @pl.when(j == last)
    def _():
        before(ext_v, pre_v, tap_v, ev, retv_o, sumv_o)
        before(ext_s, pre_s, tap_s, es, rets_o, sums_o)


def call(kernel, grid, ins, outs, scratch=(), name=None):
    def spec(shape, index):
        return pl.BlockSpec(shape, index)

    return pl.pallas_call(
        kernel,
        grid=grid,
        in_specs=[spec(s, m) for _, s, m in ins],
        out_specs=[spec(s, m) for _, _, s, m in outs],
        out_shape=[jax.ShapeDtypeStruct(full, kind) for full, kind, _, _ in outs],
        scratch_shapes=[pltpu.VMEM(s, kind) for s, kind in scratch],
        compiler_params=pltpu.CompilerParams(dimension_semantics=("arbitrary",) * len(grid)),
        name=name,
    )(*[a for a, _, _ in ins])


def passed_along(block, axis, distance):
    devices = range(lax.axis_size(axis))
    route = [(i - distance, i) for i in devices if i - distance in devices]
    return lax.ppermute(block, axis, route)


def small_sum(value, axis):
    size = lax.axis_size(axis)
    total = value
    for distance in range(1, size):
        total = total + lax.ppermute(value, axis, [(i, (i + distance) % size) for i in range(size)])
    return total


def open_pack(packed):
    state = packed[:, :STATE].astype(f32)
    decay = packed[:, STATE].astype(f32) + packed[:, STATE + 1].astype(f32)
    return state, decay[:, None]


def close_pack(state, decay):
    high = lax.reduce_precision(decay, 8, 7)
    filler = jnp.zeros((state.shape[0], PAD - 2, state.shape[2]), bf16)
    return jnp.concatenate([state.astype(bf16), high.astype(bf16), (decay - high).astype(bf16), filler], 1)


def carried_in(packed, axis, reverse):
    size, index = lax.axis_size(axis), lax.axis_index(axis)
    total, total_decay = open_pack(packed)
    prefix, prefix_decay = jnp.zeros_like(total), jnp.ones_like(total_decay)
    distance = 1
    while distance < size:
        route = [(i, i ^ distance) for i in range(size)]
        other, other_decay = open_pack(lax.ppermute(packed, axis, route))
        upper = (index // distance) % 2 == 1
        behind = jnp.logical_not(upper) if reverse else upper
        prefix = jnp.where(behind, prefix_decay * other + prefix, prefix)
        prefix_decay = jnp.where(behind, prefix_decay * other_decay, prefix_decay)
        if 2 * distance < size:
            total = jnp.where(behind, total_decay * other + total, other_decay * total + other)
            total_decay = total_decay * other_decay
            packed = close_pack(total, total_decay)
        distance *= 2
    return prefix


def body(
    hidden,
    norm_gain,
    gate_proj,
    value_proj,
    state_proj,
    step_proj,
    conv_value,
    conv_value_bias,
    conv_state,
    conv_state_bias,
    step_bias,
    decay_log,
    skip_gain,
    gate_gain,
    out_proj,
    cotangent,
):
    batch, tokens, part = hidden.shape
    head_index = lax.axis_index("head")
    ranks = lax.axis_size("head")
    features = norm_gain.shape[0]
    width, heads = value_proj.shape[1], step_proj.shape[1]
    maps = 2 * STATE
    blocks = tokens // BLOCK
    rows = batch * tokens
    count = batch * blocks
    grid = (batch, blocks)

    def row(block_width):
        return (BLOCK, block_width), lambda i, j: (i * blocks + j, 0)

    def back_row(block_width):
        return (BLOCK, block_width), lambda i, j: (i * blocks + blocks - 1 - j, 0)

    def fixed(array):
        rank = array.ndim
        return (array, array.shape, lambda i, j: (0,) * rank)

    def per_block(*tail):
        return (1,) + tail, lambda i, j: (i * blocks + j,) + (0,) * len(tail)

    def back_block(*tail):
        return (1,) + tail, lambda i, j: (i * blocks + blocks - 1 - j,) + (0,) * len(tail)

    def per_batch(*tail):
        return (1,) + tail, lambda i, j: (i,) + (0,) * len(tail)

    def lead(vector):
        return vector[None, :]

    full_rows = lax.all_gather(hidden, "head", axis=2, tiled=True)
    cot_rows = lax.all_gather(cotangent, "head", axis=2, tiled=True).reshape(rows, features)
    edge = passed_along(full_rows[:, tokens - PAD :], "seq", 1)
    full_rows = full_rows.reshape(rows, features)
    skip = lead(jnp.repeat(skip_gain, HEAD_DIM))
    bias, rate = lead(step_bias), lead(decay_log)
    gain = lead(gate_gain)

    def out(full, kind, block):
        return (full, kind) + block

    (
        normed, inv_rms, gate_in, conv_v, conv_s, mixed_v, mixed_s, x, b, c, raw, step, cum, cumt, stept,
        local, packed, edge_v, edge_s,
    ) = call(
        project_kernel,
        grid,
        [
            (full_rows,) + row(features),
            (edge,) + per_batch(PAD, features),
            fixed(lead(norm_gain)),
            fixed(gate_proj),
            fixed(value_proj),
            fixed(state_proj),
            fixed(step_proj),
            fixed(conv_value),
            fixed(lead(conv_value_bias)),
            fixed(conv_state),
            fixed(lead(conv_state_bias)),
            fixed(bias),
            fixed(rate),
        ],
        [
            out((rows, features), bf16, row(features)),
            out((rows, 128), f32, row(128)),
            out((rows, width), f32, row(width)),
            out((rows, width), f32, row(width)),
            out((rows, maps), f32, row(maps)),
            out((rows, width), f32, row(width)),
            out((rows, maps), f32, row(maps)),
            out((rows, width), bf16, row(width)),
            out((rows, STATE), bf16, row(STATE)),
            out((rows, STATE), bf16, row(STATE)),
            out((rows, heads), f32, row(heads)),
            out((rows, heads), f32, row(heads)),
            out((rows, heads), f32, row(heads)),
            out((count, heads, BLOCK), f32, per_block(heads, BLOCK)),
            out((count, heads, BLOCK), f32, per_block(heads, BLOCK)),
            out((count, STATE, width), f32, per_block(STATE, width)),
            out((batch, STATE + PAD, width), bf16, per_batch(STATE + PAD, width)),
            out((batch, EDGE, width), f32, per_batch(EDGE, width)),
            out((batch, EDGE, maps), f32, per_batch(EDGE, maps)),
        ],
        [
            ((EDGE + BLOCK, width), f32),
            ((EDGE + BLOCK, maps), f32),
            ((STATE, width), f32),
            ((1, width), f32),
        ],
        name="project",
    )
    entering = carried_in(packed, "seq", False)
    (y,) = call(
        within_kernel,
        grid,
        [
            (x,) + row(width),
            (b,) + row(STATE),
            (c,) + row(STATE),
            (cum,) + row(heads),
            (cumt,) + per_block(heads, BLOCK),
            (stept,) + per_block(heads, BLOCK),
            fixed(skip),
        ],
        [out((rows, width), f32, row(width))],
        name="within",
    )
    ssd_out, grad_normal, starts, stats = call(
        output_kernel,
        grid,
        [
            (y,) + row(width),
            (c,) + row(STATE),
            (cum,) + row(heads),
            (local,) + per_block(STATE, width),
            (entering,) + per_batch(STATE, width),
            (gate_in,) + row(width),
            (cot_rows,) + row(features),
            fixed(out_proj),
            fixed(gain),
        ],
        [
            out((rows, width), f32, row(width)),
            out((rows, width), f32, row(width)),
            out((count, STATE, width), f32, per_block(STATE, width)),
            ((8, rows), f32, (8, BLOCK), lambda i, j: (0, i * blocks + j)),
        ],
        [((STATE, width), f32)],
        name="output",
    )
    stats = small_sum(stats, "head")
    normal_gated, grad_ssd, grad_gate_in, row_term, state_grads, gate_sums, packed_back = call(
        partial(gate_kernel, float(width * ranks)),
        grid,
        [
            (ssd_out,) + row(width),
            (gate_in,) + row(width),
            (grad_normal,) + row(width),
            (stats, (8, BLOCK), lambda i, j: (0, i * blocks + j)),
            fixed(gain),
            fixed(skip),
            (x,) + row(width),
            (c,) + row(STATE),
            (cum,) + row(heads),
        ],
        [
            out((rows, width), bf16, row(width)),
            out((rows, width), bf16, row(width)),
            out((rows, width), bf16, row(width)),
            out((rows, heads), f32, row(heads)),
            out((count, STATE, width), f32, per_block(STATE, width)),
            ((8, width), f32, (8, width), lambda i, j: (0, 0)),
            out((batch, STATE + PAD, width), bf16, per_batch(STATE + PAD, width)),
        ],
        [((STATE, width), f32), ((1, width), f32)],
        name="gate",
    )
    leaving = carried_in(packed_back, "seq", True)
    grad_x_in, grad_b_in, grad_c_in = call(
        score_kernel,
        grid,
        [
            (x,) + row(width),
            (b,) + row(STATE),
            (c,) + row(STATE),
            (cum,) + row(heads),
            (cumt,) + per_block(heads, BLOCK),
            (step,) + row(heads),
            (grad_ssd,) + row(width),
        ],
        [
            out((rows, width), f32, row(width)),
            out((rows, STATE), f32, row(STATE)),
            out((rows, STATE), f32, row(STATE)),
        ],
        [((BLOCK, BLOCK), f32)],
        name="score",
    )
    partial_out = dot(normal_gated, out_proj).astype(bf16).reshape(batch, tokens, features)
    out_part = lax.psum_scatter(partial_out, "head", scatter_dimension=2, tiled=True)
    block_out = (hidden.astype(f32) + out_part.astype(f32)).astype(bf16)
    out_proj_grad = lax.psum(dot(normal_gated, cot_rows, TN).astype(bf16), "seq")
    gate_proj_part = dot(normed, grad_gate_in, TN).astype(bf16)
    gate_proj_grad = lax.psum(gate_proj_part, "seq")

    (
        grad_conv_v, grad_conv_s, tail_v, tail_s, ret_v, ret_s, grad_raw, sum_v, sum_s, sum_h,
    ) = call(
        back_kernel,
        grid,
        [
            (leaving,) + per_batch(STATE, width),
            (starts,) + back_block(STATE, width),
            (state_grads,) + back_block(STATE, width),
            (grad_x_in,) + back_row(width),
            (grad_b_in,) + back_row(STATE),
            (grad_c_in,) + back_row(STATE),
            (row_term,) + back_row(heads),
            (x,) + back_row(width),
            (grad_ssd,) + back_row(width),
            (b,) + back_row(STATE),
            (c,) + back_row(STATE),
            (raw,) + back_row(heads),
            (step,) + back_row(heads),
            (cum,) + back_row(heads),
            (mixed_v,) + back_row(width),
            (mixed_s,) + back_row(maps),
            (conv_v,) + back_row(width),
            (conv_s,) + back_row(maps),
            (edge_v,) + per_batch(EDGE, width),
            (edge_s,) + per_batch(EDGE, maps),
            fixed(conv_value),
            fixed(conv_state),
            fixed(skip),
            fixed(bias),
            fixed(rate),
        ],
        [
            out((rows, width), bf16, back_row(width)),
            out((rows, maps), bf16, back_row(maps)),
            out((batch, PAD, width), f32, per_batch(PAD, width)),
            out((batch, PAD, maps), f32, per_batch(PAD, maps)),
            out((batch, EDGE, width), f32, per_batch(EDGE, width)),
            out((batch, EDGE, maps), f32, per_batch(EDGE, maps)),
            out((rows, heads), bf16, back_row(heads)),
            ((8, width), f32, (8, width), lambda i, j: (0, 0)),
            ((8, maps), f32, (8, maps), lambda i, j: (0, 0)),
            ((8, heads), f32, (8, heads), lambda i, j: (0, 0)),
        ],
        [
            ((STATE, width), f32),
            ((BLOCK + EDGE, width), f32),
            ((BLOCK + EDGE, maps), f32),
            ((2 * EDGE, width), f32),
            ((2 * EDGE, maps), f32),
        ],
        name="back",
    )
    back_edge = passed_along(jnp.concatenate([ret_v, ret_s], 2), "seq", -1)

    def mended(grad, tail, given):
        lower = (tail[:, PAD - EDGE :] + given).astype(bf16)
        tail = jnp.concatenate([tail[:, : PAD - EDGE].astype(bf16), lower], 1)
        grad = grad.reshape(batch, tokens, -1)
        return lax.dynamic_update_slice(grad, tail, (0, tokens - PAD, 0)).reshape(rows, -1)

    grad_conv_v = mended(grad_conv_v, tail_v, back_edge[..., :width])
    grad_conv_s = mended(grad_conv_s, tail_s, back_edge[..., width:])

    grad_normed = (
        dot(grad_gate_in, gate_proj, NT)
        + dot(grad_conv_v, value_proj, NT)
        + dot(grad_conv_s, state_proj, NT)
        + dot(grad_raw, step_proj, NT)
    ).astype(bf16)
    grad_part = lax.psum_scatter(
        grad_normed.reshape(batch, tokens, features), "head", scatter_dimension=2, tiled=True
    ).astype(f32)

    value_part = dot(normed, grad_conv_v, TN).astype(bf16)
    state_part = dot(normed, grad_conv_s, TN).astype(bf16)
    step_part = dot(normed, grad_raw, TN)
    value_proj_grad = lax.psum(value_part, "seq")
    state_proj_grad = lax.psum(state_part, ("seq", "head"))

    def along(left, right):
        return jnp.sum(left.astype(f32) * right, -1)

    row_dot = along(grad_gate_in, gate_in) + along(grad_conv_v, conv_v) + along(grad_conv_s, conv_s)
    row_dot = (row_dot + along(grad_raw, raw)) / features
    row_dot = lax.psum(row_dot, "head").reshape(batch, tokens, 1)

    inv = inv_rms[:, :1].reshape(batch, tokens, 1)
    unit = hidden.astype(f32) * inv
    norm_part = jnp.sum(grad_part * unit, (0, 1))
    gain_part = lax.dynamic_slice_in_dim(norm_gain, head_index * part, part)
    grad_input = inv * (grad_part * gain_part - unit * row_dot)
    hidden_grad = (cotangent.astype(f32) + grad_input).astype(bf16)

    sum_s = lax.psum(sum_s, "head")
    totals = lax.psum(
        (norm_part, step_part, sum_v, sum_s, sum_h, gate_sums),
        "seq",
    )
    norm_gain_grad, step_proj_grad, sum_v, sum_s, sum_h, gate_sums = totals
    return (
        block_out,
        hidden_grad,
        norm_gain_grad,
        gate_proj_grad.astype(f32),
        value_proj_grad.astype(f32),
        state_proj_grad.astype(f32),
        step_proj_grad,
        sum_v[:CONV],
        sum_v[CONV],
        sum_s[:CONV],
        sum_s[CONV],
        sum_h[0],
        sum_h[1],
        jnp.sum(gate_sums[1].reshape(heads, HEAD_DIM), -1),
        gate_sums[0],
        out_proj_grad.astype(f32),
    )


def solution(mesh):
    placed = (
        P(None, "seq", "head"),
        P(),
        P(None, "head"),
        P(None, "head"),
        P(),
        P(None, "head"),
        P(None, "head"),
        P("head"),
        P(),
        P(),
        P("head"),
        P("head"),
        P("head"),
        P("head"),
        P("head", None),
        P(None, "seq", "head"),
    )
    return jax.shard_map(
        body,
        mesh=mesh,
        in_specs=placed,
        out_specs=(
            P(None, "seq", "head"),
            P(None, "seq", "head"),
            P("head"),
            P(None, "head"),
            P(None, "head"),
            P(),
            P(None, "head"),
            P(None, "head"),
            P("head"),
            P(),
            P(),
            P("head"),
            P("head"),
            P("head"),
            P("head"),
            P("head", None),
        ),
        check_vma=False,
    )
```

```python
from functools import partial

import jax
import jax.numpy as jnp
from jax import lax
from jax.experimental import pallas as pl
from jax.experimental.pallas import tpu as pltpu
from jax.sharding import PartitionSpec as P

HEAD_DIM = 64
STATE = 128
CONV = 4
BLOCK = 256
EPS = 1e-05
EDGE = 8
PAD = 16

bf16 = jnp.bfloat16
f32 = jnp.float32

NN = (((1,), (0,)), ((), ()))
NT = (((1,), (1,)), ((), ()))
TN = (((0,), (0,)), ((), ()))


def dot(left, right, dims=NN):
    return lax.dot_general(left, right, dims, preferred_element_type=f32)


def parts_of(value, count):
    parts, rest = [], value
    for _ in range(count - 1):
        part = rest.astype(bf16)
        parts.append(part)
        rest = rest - part.astype(f32)
    parts.append(rest.astype(bf16))
    return parts


def head_map(heads, width):
    head = lax.broadcasted_iota(jnp.int32, (heads, width), 0)
    channel = lax.broadcasted_iota(jnp.int32, (heads, width), 1)
    return ((channel >> 6) == head).astype(bf16)


def spread(value, hmap, count=2):
    return sum(dot(part, hmap) for part in parts_of(value, count))


def per_head(value, hmap, count=2):
    return sum(dot(part, hmap, NT) for part in parts_of(value, count))


def triangle(lower):
    row = lax.broadcasted_iota(jnp.int32, (BLOCK, BLOCK), 0)
    col = lax.broadcasted_iota(jnp.int32, (BLOCK, BLOCK), 1)
    return (row >= col) if lower else (row <= col)


def running_sum(value, lower):
    tri = jnp.where(triangle(lower), 1.0, 0.0).astype(bf16)
    return sum(dot(tri, part) for part in parts_of(value, 3))


def sigmoid(value):
    return 1.0 / (1.0 + jnp.exp(-value))


def softplus(value):
    return jnp.maximum(value, 0.0) + jnp.log1p(jnp.exp(-jnp.abs(value)))


def silu_slope(value):
    sigma = sigmoid(value)
    return sigma * (1.0 + value * (1.0 - sigma))


def shifted_taps(source, taps, start, rows):
    return sum(taps[k : k + 1, :] * source[pl.ds(start + k, rows), :] for k in range(CONV))


def pack_state(out, state, decay):
    out[0, :STATE, :] = state
    high = decay.astype(bf16)
    rest = (decay - high.astype(f32)).astype(bf16)
    row = lax.broadcasted_iota(jnp.int32, (PAD, state.shape[1]), 0)
    tail = jnp.where(row == 0, high.astype(f32), jnp.where(row == 1, rest.astype(f32), 0.0))
    out[0, STATE:, :] = tail


def project_kernel(
    rows, edge, gain, gate_w, value_w, state_w, step_w, tap_v, bias_v, tap_s, bias_s, step_bias, decay_log,
    normed_o, inv_o, gate_o, conv_o, mixed_o, x_o, b_o, c_o, raw_o, step_o, cum_o, cumt_o, stept_o,
    local_o, pack_o, edge_o,
    ext_v, ext_s, held, factor,
):
    j, last = pl.program_id(1), pl.num_programs(1) - 1
    heads, width = step_w.shape[1], value_w.shape[1]
    hmap = head_map(heads, width)

    def norm(block):
        block = block.astype(f32)
        inv = lax.rsqrt(jnp.mean(block * block, -1, keepdims=True) + EPS)
        return (block * inv * gain[...]).astype(bf16), inv

    @pl.when(j == 0)
    def _():
        before, _ = norm(edge[0])
        edge_v = dot(before, value_w[...])[PAD - EDGE :]
        edge_s = dot(before, state_w[...])[PAD - EDGE :]
        ext_v[:EDGE, :] = edge_v
        ext_s[:EDGE, :] = edge_s
        edge_o[0, :, :width] = edge_v
        edge_o[0, :, width:] = edge_s
        held[...] = jnp.zeros_like(held)
        factor[...] = jnp.ones_like(factor)

    @pl.when(j > 0)
    def _():
        ext_v[:EDGE, :] = ext_v[BLOCK:, :]
        ext_s[:EDGE, :] = ext_s[BLOCK:, :]

    normed, inv = norm(rows[...])
    normed_o[...] = normed
    inv_o[...] = jnp.broadcast_to(inv, inv_o.shape)
    gate_o[...] = dot(normed, gate_w[...])
    conv_v = dot(normed, value_w[...])
    conv_s = dot(normed, state_w[...])
    raw = dot(normed, step_w[...])
    conv_o[:, :width] = conv_v
    conv_o[:, width:] = conv_s
    ext_v[EDGE:, :] = conv_v
    ext_s[EDGE:, :] = conv_s
    mixed_v = bias_v[...] + shifted_taps(ext_v, tap_v, EDGE - CONV + 1, BLOCK)
    mixed_s = bias_s[...] + shifted_taps(ext_s, tap_s, EDGE - CONV + 1, BLOCK)
    mixed_o[:, :width] = mixed_v
    mixed_o[:, width:] = mixed_s
    x = (mixed_v * sigmoid(mixed_v)).astype(bf16)
    maps = (mixed_s * sigmoid(mixed_s)).astype(bf16)
    x_o[...] = x
    b_o[...] = maps[:, :STATE]
    c_o[...] = maps[:, STATE:]

    step = softplus(raw + step_bias[...])
    cum = running_sum(-jnp.exp(decay_log[...]) * step, True)
    raw_o[...] = raw
    step_o[...] = step
    cum_o[...] = cum
    cumt_o[0] = cum.T
    stept_o[0] = step.T
    total = cum[BLOCK - 1 :]
    weights = jnp.exp(total - cum) * step
    x_weighted = (x.astype(f32) * spread(weights, hmap)).astype(bf16)
    local = dot(maps[:, :STATE], x_weighted, TN)
    local_o[0] = local
    decay = spread(jnp.exp(cum[BLOCK - 8 :]), hmap)[7:]
    held[...] = decay * held[...] + local
    factor[...] = decay * factor[...]

    @pl.when(j == last)
    def _():
        pack_state(pack_o, held[...], factor[...])


def within_kernel(x, b, c, cum, cumt, stept, skip, y_o):
    heads, width = cum.shape[1], x.shape[1]
    hmap = head_map(heads, width)
    causal = triangle(True)
    scores = dot(c[...], b[...], NT)
    left = lax.broadcasted_iota(jnp.int32, (BLOCK, 2 * HEAD_DIM), 1) < HEAD_DIM
    for pair in range(heads // 2):
        lanes = slice(pair * 2 * HEAD_DIM, (pair + 1) * 2 * HEAD_DIM)
        x_pair = x[:, lanes]
        inside = []
        for h in (2 * pair, 2 * pair + 1):
            spread_h = jnp.where(causal, cum[:, h : h + 1] - cumt[0, h : h + 1, :], -1e30)
            mixing = (scores * jnp.exp(spread_h) * stept[0, h : h + 1, :]).astype(bf16)
            inside.append(dot(mixing, x_pair))
        y_o[:, lanes] = jnp.where(left, inside[0], inside[1]) + skip[:, lanes] * x_pair.astype(f32)


def row_sum(value):
    ones = jnp.ones((8, value.shape[1]), bf16)
    return sum(dot(ones, part, NT) for part in parts_of(value, 3))


def output_kernel(y, c, cum, local, entering, gate, gate_gain, ssd_o, scaled_o, starts_o, square_o, state):
    heads, width = cum.shape[1], gate.shape[1]
    hmap = head_map(heads, width)

    @pl.when(pl.program_id(1) == 0)
    def _():
        state[...] = entering[0]

    start = state[...]
    starts_o[0] = start
    scale = spread(jnp.exp(cum[BLOCK - 8 :, :]), hmap)[7:]
    low = start.astype(bf16)
    lift, c_float = jnp.exp(cum[...]), c[...].astype(f32)
    left = lax.broadcasted_iota(jnp.int32, (BLOCK, 2 * HEAD_DIM), 1) < HEAD_DIM
    for pair in range(heads // 2):
        lanes = slice(pair * 2 * HEAD_DIM, (pair + 1) * 2 * HEAD_DIM)
        carried = [
            dot((lift[:, h : h + 1] * c_float).astype(bf16), low[:, lanes]) for h in (2 * pair, 2 * pair + 1)
        ]
        ssd_o[:, lanes] = y[:, lanes] + jnp.where(left, carried[0], carried[1])
    ssd = ssd_o[...]
    state[...] = scale * start + local[0]
    gate_in = gate[...]
    gated = ssd * (gate_in * sigmoid(gate_in))
    scaled_o[...] = gated * gate_gain[...]
    square_o[...] = row_sum(gated * gated)


def product_kernel(cot, out_w, scaled, square, grad_o, stats_o):
    grad = dot(cot[...], out_w[...], NT)
    grad_o[...] = grad
    first = lax.broadcasted_iota(jnp.int32, (8, BLOCK), 0) == 0
    stats_o[...] = jnp.where(first, square[...], row_sum(grad * scaled[...]))


def gate_kernel(
    inner, ssd, gate, grad, stats, gate_gain, skip, x, c, cum,
    normal_o, gssd_o, ggate_o, row_o, sgrad_o, sums_o, pack_o, held, factor,
):
    i, j, last = pl.program_id(0), pl.program_id(1), pl.num_programs(1) - 1
    heads, width = cum.shape[1], gate.shape[1]
    hmap = head_map(heads, width)

    @pl.when((i == 0) & (j == 0))
    def _():
        sums_o[...] = jnp.zeros_like(sums_o)

    @pl.when(j == 0)
    def _():
        held[...] = jnp.zeros_like(held)
        factor[...] = jnp.ones_like(factor)

    columns = stats[...].T
    inv_gate = lax.rsqrt(columns[:, 0:1] / inner + EPS)
    mean_dot = inv_gate * columns[:, 1:2] / inner
    gate_in, ssd_out = gate[...], ssd[...]
    sigma = sigmoid(gate_in)
    act = gate_in * sigma
    unit = ssd_out * act * inv_gate
    normal_o[...] = (unit * gate_gain[...]).astype(bf16)
    grad_normal = grad[...]
    grad_gated = inv_gate * (grad_normal * gate_gain[...] - unit * mean_dot)
    grad_ssd = (grad_gated * act).astype(bf16)
    gssd_o[...] = grad_ssd
    ggate_o[...] = (grad_gated * ssd_out * (sigma * (1.0 + gate_in * (1.0 - sigma)))).astype(bf16)
    grad_float, x_float = grad_ssd.astype(f32), x[...].astype(f32)
    row_o[...] = per_head(grad_float * (ssd_out - skip[...] * x_float), hmap)
    gain_sum = jnp.sum(grad_normal * unit, 0, keepdims=True)
    skip_sum = jnp.sum(grad_float * x_float, 0, keepdims=True)
    row = lax.broadcasted_iota(jnp.int32, (8, width), 0)
    sums_o[...] += jnp.where(row == 0, gain_sum, jnp.where(row == 1, skip_sum, 0.0))
    scale = spread(jnp.exp(cum[BLOCK - 8 :, :]), hmap)[7:]
    lift, c_float = jnp.exp(cum[...]), c[...].astype(f32)
    left = lax.broadcasted_iota(jnp.int32, (STATE, 2 * HEAD_DIM), 1) < HEAD_DIM
    for pair in range(heads // 2):
        lanes = slice(pair * 2 * HEAD_DIM, (pair + 1) * 2 * HEAD_DIM)
        found = [
            dot((lift[:, h : h + 1] * c_float).astype(bf16), grad_ssd[:, lanes], TN) for h in (2 * pair, 2 * pair + 1)
        ]
        sgrad_o[0, :, lanes] = jnp.where(left, found[0], found[1])
    held[...] += factor[...] * sgrad_o[0]
    factor[...] = factor[...] * scale

    @pl.when(j == last)
    def _():
        pack_state(pack_o, held[...], factor[...])


def score_kernel(x, b, c, cum, cumt, step, gssd, gx_o, gb_o, gc_o, total):
    heads = cum.shape[1]
    causal = triangle(False)
    scores = dot(b[...], c[...], NT)
    left = lax.broadcasted_iota(jnp.int32, (BLOCK, 2 * HEAD_DIM), 1) < HEAD_DIM
    zero = jnp.zeros((BLOCK, 2 * HEAD_DIM), bf16)
    for pair in range(heads // 2):
        lanes = slice(pair * 2 * HEAD_DIM, (pair + 1) * 2 * HEAD_DIM)
        x_pair, g_pair = x[:, lanes], gssd[:, lanes]
        inside = []
        for side in range(2):
            h = 2 * pair + side
            spread_h = jnp.where(causal, cumt[0, h : h + 1, :] - cum[:, h : h + 1], -1e30)
            damping = jnp.exp(spread_h) * step[:, h : h + 1]
            x_head = jnp.where(left, x_pair, zero) if side == 0 else jnp.where(left, zero, x_pair)
            low = (dot(x_head, g_pair, NT) * damping).astype(bf16).astype(f32)
            if h == 0:
                total[...] = low
            else:
                total[...] += low
            inside.append(dot((scores * damping).astype(bf16), g_pair))
        gx_o[:, lanes] = jnp.where(left, inside[0], inside[1])
    high, rest = parts_of(total[...], 2)
    gb_o[...] = dot(high, c[...]) + dot(rest, c[...])
    gc_o[...] = dot(high, b[...], TN) + dot(rest, b[...], TN)


def back_kernel(
    leaving, starts, sgrad, gx_in, gb_in, gc_in, row_term, x, gssd, b, c, raw, step, cum,
    mixed, conv, edge, taps, skip, step_bias, decay_log,
    grad_o, tail_o, ret_o, graw_o, sum_o, sumh_o,
    end, ext, pre,
):
    i, j, last = pl.program_id(0), pl.program_id(1), pl.num_programs(1) - 1
    heads, width = cum.shape[1], x.shape[1]
    hmap = head_map(heads, width)
    place = lax.broadcasted_iota(jnp.int32, sum_o.shape, 0)

    @pl.when((i == 0) & (j == 0))
    def _():
        sum_o[...] = jnp.zeros_like(sum_o)
        sumh_o[...] = jnp.zeros_like(sumh_o)

    @pl.when(j == 0)
    def _():
        end[...] = leaving[0]
        ext[BLOCK:, :] = jnp.zeros((EDGE, ext.shape[1]), f32)

    @pl.when(j > 0)
    def _():
        ext[BLOCK:, :] = ext[:EDGE, :]

    end_grad = end[...]
    end_low = end_grad.astype(bf16)
    start = starts[0]
    cum_v, step_v = cum[...], step[...]
    x_float, g_float = x[...].astype(f32), gssd[...].astype(f32)
    remain = jnp.exp(cum_v[BLOCK - 1 :] - cum_v)
    weight = spread(remain * step_v, hmap)
    scale = spread(jnp.exp(cum_v), hmap)
    decay = scale[BLOCK - 1 :]
    grad_weighted = weight * dot(b[...], end_low)
    q_weight = per_head(x_float * grad_weighted, hmap)
    q_mixing = per_head(x_float * gx_in[...], hmap)
    grad_x = gx_in[...] + grad_weighted + skip[...] * g_float
    x_weighted = (x_float * weight).astype(bf16)
    grad_b = gb_in[...] + dot(x_weighted, end_low, NT)
    grad_c = gc_in[...] + sum(dot(part, start.astype(bf16), NT) for part in parts_of(g_float * scale, 2))
    along = jnp.sum(end_grad * start, 0, keepdims=True) * decay
    grad_total = per_head(jnp.broadcast_to(along, (8, width)), hmap)[:1] + jnp.sum(q_weight, 0, keepdims=True)
    end[...] = decay * end_grad + sgrad[0]

    final = lax.broadcasted_iota(jnp.int32, (BLOCK, heads), 0) == BLOCK - 1
    grad_cum = row_term[...] - q_mixing - q_weight + jnp.where(final, grad_total, 0.0)
    grad_log = running_sum(grad_cum, False)
    rate = -jnp.exp(decay_log[...])
    shifted = raw[...] + step_bias[...]
    sigma = sigmoid(shifted)
    ratio = jnp.where(step_v > 0.0, sigma / jnp.where(step_v > 0.0, step_v, 1.0), 1.0)
    grad_raw = grad_log * rate * sigma + (q_mixing + q_weight) * ratio
    graw_o[...] = grad_raw.astype(bf16)
    bias_sum = jnp.sum(grad_raw, 0, keepdims=True)
    decay_sum = jnp.sum(grad_log * rate * step_v, 0, keepdims=True)
    row = lax.broadcasted_iota(jnp.int32, (8, heads), 0)
    sumh_o[...] += jnp.where(row == 0, bias_sum, jnp.where(row == 1, decay_sum, 0.0))

    ext[:BLOCK, :width] = grad_x * silu_slope(mixed[:, :width])
    slope = silu_slope(mixed[:, width:])
    ext[:BLOCK, width : width + STATE] = grad_b * slope[:, :STATE]
    ext[:BLOCK, width + STATE :] = grad_c * slope[:, STATE:]

    views = [ext[pl.ds(CONV - 1 - k, BLOCK), :] for k in range(CONV)]
    grad = sum(taps[k : k + 1, :] * views[k] for k in range(CONV))
    grad_o[...] = grad.astype(bf16)

    @pl.when(j == 0)
    def _():
        tail_o[0] = grad[BLOCK - PAD :]

    lines = [jnp.sum(conv[...] * view, 0, keepdims=True) for view in views]
    lines.append(jnp.sum(ext[:BLOCK, :], 0, keepdims=True))
    sum_o[...] += sum(jnp.where(place == k, line, 0.0) for k, line in enumerate(lines))

    @pl.when(j == last)
    def _():
        pre[:EDGE, :] = jnp.zeros((EDGE, pre.shape[1]), f32)
        pre[EDGE:, :] = ext[:EDGE, :]
        early = [pre[pl.ds(CONV - 1 - k, EDGE), :] for k in range(CONV)]
        ret_o[0] = sum(taps[k : k + 1, :] * early[k] for k in range(CONV))
        sum_o[...] += sum(
            jnp.where(place == k, jnp.sum(edge[0] * early[k], 0, keepdims=True), 0.0) for k in range(CONV)
        )


def outer_kernel(split, left, right, out):
    whole = dot(left[...], right[...], TN)
    high = whole.astype(bf16)
    width = whole.shape[1]
    out[:, :width] = high
    if split:
        out[:, width:] = (whole[:, width - split :] - high[:, width - split :].astype(f32)).astype(bf16)


def outer(left, right, size, steps, at=0, split=0):
    rows, width = right.shape
    lines = size // steps
    return pl.pallas_call(
        lambda where, *refs: outer_kernel(split, *refs),
        grid_spec=pltpu.PrefetchScalarGridSpec(
            num_scalar_prefetch=1,
            grid=(steps,),
            in_specs=[
                pl.BlockSpec((rows, lines), lambda i, where: (0, where[0] * steps + i)),
                pl.BlockSpec((rows, width), lambda i, where: (0, 0)),
            ],
            out_specs=pl.BlockSpec((lines, width + split), lambda i, where: (i, 0)),
        ),
        out_shape=jax.ShapeDtypeStruct((size, width + split), bf16),
        compiler_params=pltpu.CompilerParams(dimension_semantics=("arbitrary",)),
    )(jnp.asarray(at, jnp.int32).reshape(1), left, right)


def call(kernel, grid, ins, outs, scratch=()):
    def spec(shape, index):
        return pl.BlockSpec(shape, index)

    return pl.pallas_call(
        kernel,
        grid=grid,
        in_specs=[spec(s, m) for _, s, m in ins],
        out_specs=[spec(s, m) for _, _, s, m in outs],
        out_shape=[jax.ShapeDtypeStruct(full, kind) for full, kind, _, _ in outs],
        scratch_shapes=[pltpu.VMEM(s, kind) for s, kind in scratch],
        compiler_params=pltpu.CompilerParams(dimension_semantics=("arbitrary",) * len(grid)),
    )(*[a for a, _, _ in ins])


def passed_along(block, axis, distance):
    devices = range(lax.axis_size(axis))
    route = [(i - distance, i) for i in devices if i - distance in devices]
    return lax.ppermute(block, axis, route)


def small_sum(value, axis):
    size = lax.axis_size(axis)
    total = value.astype(f32)
    for distance in range(1, size):
        other = lax.ppermute(value, axis, [(i, (i + distance) % size) for i in range(size)])
        total = total + other.astype(f32)
    return total


def sent(value, axis, mask):
    return lax.ppermute(value, axis, [(i, i ^ mask) for i in range(lax.axis_size(axis))])


def ordered_kernel(count, where, *refs):
    pieces, out = refs[:count], refs[count]
    turn = pl.program_id(0)
    for k, piece in enumerate(pieces):

        @pl.when(turn == k)
        def _():
            out[...] = piece[...]


def ordered(pieces, places):
    size, width = pieces[0].shape
    count = len(pieces)
    return pl.pallas_call(
        partial(ordered_kernel, count),
        grid_spec=pltpu.PrefetchScalarGridSpec(
            num_scalar_prefetch=1,
            grid=(count,),
            in_specs=[pl.BlockSpec((size, width), lambda turn, where: (0, 0))] * count,
            out_specs=pl.BlockSpec((size, width), lambda turn, where: (where[turn], 0)),
        ),
        out_shape=jax.ShapeDtypeStruct((count * size, width), pieces[0].dtype),
        compiler_params=pltpu.CompilerParams(dimension_semantics=("arbitrary",)),
        name="ordered",
    )(places.astype(jnp.int32), *pieces)


def join_kernel(where, own, other, *outs):
    def give(piece):
        start = 0
        for out in outs:
            out[...] = piece[:, start : start + out.shape[1]].astype(f32)
            start += out.shape[1]

    @pl.when(pl.program_id(0) == 0)
    def _():
        give(own)

    @pl.when(pl.program_id(0) == 1)
    def _():
        give(other)


def joined(own, other, upper, widths):
    size, width = own.shape
    steps = 2
    lines = size // steps
    return pl.pallas_call(
        join_kernel,
        grid_spec=pltpu.PrefetchScalarGridSpec(
            num_scalar_prefetch=1,
            grid=(2, steps),
            in_specs=[
                pl.BlockSpec((lines, width), lambda turn, i, where: (jnp.where(turn == 0, i, steps - 1), 0)),
                pl.BlockSpec((lines, width), lambda turn, i, where: (jnp.where(turn == 0, 0, i), 0)),
            ],
            out_specs=[
                pl.BlockSpec((lines, part), lambda turn, i, where: ((where[0] ^ turn) * steps + i, 0))
                for part in widths
            ],
        ),
        out_shape=[jax.ShapeDtypeStruct((2 * size, part), f32) for part in widths],
        compiler_params=pltpu.CompilerParams(dimension_semantics=("arbitrary",) * 2),
        name="join",
    )(upper.astype(jnp.int32)[None], own, other)


def chunk_kernel(
    ranks, gate_g, conv_g, step_g, normed, inv, gain, gate_w, value_w, state_w, step_w, out, sums_o
):
    part, width = out.shape[2], value_w.shape[1]
    grads = (gate_g[...], conv_g[:, :width], conv_g[:, width:], step_g[...])
    weights = (gate_w, value_w, state_w, step_w)
    whole = sum(dot(g, w[...], NT) for g, w in zip(grads, weights))
    rows = normed[...].astype(f32)
    product = whole * rows
    mean_dot = jnp.mean(product, -1, keepdims=True)
    whole = (inv[:, :1] * (whole * gain[...] - rows / gain[...] * mean_dot)).astype(bf16)
    for k in range(ranks):
        out[k] = whole[:, k * part : (k + 1) * part]

    @pl.when((pl.program_id(0) == 0) & (pl.program_id(1) == 0))
    def _():
        sums_o[...] = jnp.zeros_like(sums_o)

    first = lax.broadcasted_iota(jnp.int32, sums_o.shape, 0) == 0
    sums_o[...] += jnp.where(first, jnp.sum(product, 0, keepdims=True) / gain[...], 0.0)


def result_kernel(ranks, left, right, out):
    part = out.shape[2]
    whole = dot(left[...], right[...]).astype(bf16)
    for k in range(ranks):
        out[k] = whole[:, k * part : (k + 1) * part]


def open_pack(packed):
    state = packed[:, :STATE].astype(f32)
    decay = packed[:, STATE].astype(f32) + packed[:, STATE + 1].astype(f32)
    return state, decay[:, None]


def close_pack(state, decay):
    high = lax.reduce_precision(decay, 8, 7)
    filler = jnp.zeros((state.shape[0], PAD - 2, state.shape[2]), bf16)
    return jnp.concatenate([state.astype(bf16), high.astype(bf16), (decay - high).astype(bf16), filler], 1)


def carried_in(packed, axis, reverse):
    size, index = lax.axis_size(axis), lax.axis_index(axis)
    total, total_decay = open_pack(packed)
    prefix, prefix_decay = jnp.zeros_like(total), jnp.ones_like(total_decay)
    distance = 1
    while distance < size:
        route = [(i, i ^ distance) for i in range(size)]
        given = lax.ppermute(packed, axis, route)
        other, other_decay = open_pack(given)
        upper = (index // distance) % 2 == 1
        behind = jnp.logical_not(upper) if reverse else upper
        prefix = jnp.where(behind, prefix_decay * other + prefix, prefix)
        prefix_decay = jnp.where(behind, prefix_decay * other_decay, prefix_decay)
        if 2 * distance < size:
            total = jnp.where(behind, total_decay * other + total, other_decay * total + other)
            total_decay = total_decay * other_decay
            packed = close_pack(total, total_decay)
        distance = 2 * distance
    return prefix


def body(
    hidden,
    norm_gain,
    gate_proj,
    value_proj,
    state_proj,
    step_proj,
    conv_value,
    conv_value_bias,
    conv_state,
    conv_state_bias,
    step_bias,
    decay_log,
    skip_gain,
    gate_gain,
    out_proj,
    cotangent,
):
    batch, tokens, part = hidden.shape
    head_index = lax.axis_index("head")
    ranks = lax.axis_size("head")
    features = norm_gain.shape[0]
    width, heads = value_proj.shape[1], step_proj.shape[1]
    maps = 2 * STATE
    blocks = tokens // BLOCK
    rows = batch * tokens
    count = batch * blocks
    grid = (batch, blocks)

    def row(block_width):
        return (BLOCK, block_width), lambda i, j: (i * blocks + j, 0)

    def back_row(block_width):
        return (BLOCK, block_width), lambda i, j: (i * blocks + blocks - 1 - j, 0)

    def fixed(array):
        rank = array.ndim
        return (array, array.shape, lambda i, j: (0,) * rank)

    def per_block(*tail):
        return (1,) + tail, lambda i, j: (i * blocks + j,) + (0,) * len(tail)

    def back_block(*tail):
        return (1,) + tail, lambda i, j: (i * blocks + blocks - 1 - j,) + (0,) * len(tail)

    def per_batch(*tail):
        return (1,) + tail, lambda i, j: (i,) + (0,) * len(tail)

    def lead(vector):
        return vector[None, :]

    full_rows = lax.all_gather(hidden, "head", axis=2, tiled=True)
    cot_rows = lax.all_gather(cotangent, "head", axis=2, tiled=True).reshape(rows, features)
    edge = passed_along(full_rows[:, tokens - PAD :], "seq", 1)
    full_rows = full_rows.reshape(rows, features)
    skip = lead(jnp.repeat(skip_gain, HEAD_DIM))
    bias, rate = lead(step_bias), lead(decay_log)
    gain = lead(gate_gain)

    def out(full, kind, block):
        return (full, kind) + block

    (
        normed, inv_rms, gate_in, conv_in, mixed, x, b, c, raw, step, cum, cumt, stept,
        local, packed, conv_edge,
    ) = call(
        project_kernel,
        grid,
        [
            (full_rows,) + row(features),
            (edge,) + per_batch(PAD, features),
            fixed(lead(norm_gain)),
            fixed(gate_proj),
            fixed(value_proj),
            fixed(state_proj),
            fixed(step_proj),
            fixed(conv_value),
            fixed(lead(conv_value_bias)),
            fixed(conv_state),
            fixed(lead(conv_state_bias)),
            fixed(bias),
            fixed(rate),
        ],
        [
            out((rows, features), bf16, row(features)),
            out((rows, 128), f32, row(128)),
            out((rows, width), f32, row(width)),
            out((rows, width + maps), f32, row(width + maps)),
            out((rows, width + maps), f32, row(width + maps)),
            out((rows, width), bf16, row(width)),
            out((rows, STATE), bf16, row(STATE)),
            out((rows, STATE), bf16, row(STATE)),
            out((rows, heads), f32, row(heads)),
            out((rows, heads), f32, row(heads)),
            out((rows, heads), f32, row(heads)),
            out((count, heads, BLOCK), f32, per_block(heads, BLOCK)),
            out((count, heads, BLOCK), f32, per_block(heads, BLOCK)),
            out((count, STATE, width), f32, per_block(STATE, width)),
            out((batch, STATE + PAD, width), f32, per_batch(STATE + PAD, width)),
            out((batch, EDGE, width + maps), f32, per_batch(EDGE, width + maps)),
        ],
        [
            ((EDGE + BLOCK, width), f32),
            ((EDGE + BLOCK, maps), f32),
            ((STATE, width), f32),
            ((1, width), f32),
        ],
    )
    entering = carried_in(packed, "seq", False)
    (y,) = call(
        within_kernel,
        grid,
        [
            (x,) + row(width),
            (b,) + row(STATE),
            (c,) + row(STATE),
            (cum,) + row(heads),
            (cumt,) + per_block(heads, BLOCK),
            (stept,) + per_block(heads, BLOCK),
            fixed(skip),
        ],
        [out((rows, width), f32, row(width))],
    )
    stat_row = (8, BLOCK), lambda i, j: (0, i * blocks + j)
    ssd_out, scaled, starts, square = call(
        output_kernel,
        grid,
        [
            (y,) + row(width),
            (c,) + row(STATE),
            (cum,) + row(heads),
            (local,) + per_block(STATE, width),
            (entering,) + per_batch(STATE, width),
            (gate_in,) + row(width),
            fixed(gain),
        ],
        [
            out((rows, width), f32, row(width)),
            out((rows, width), f32, row(width)),
            out((count, STATE, width), f32, per_block(STATE, width)),
            out((8, rows), f32, stat_row),
        ],
        [((STATE, width), f32)],
    )
    grad_normal, stats = call(
        product_kernel,
        grid,
        [(cot_rows,) + row(features), fixed(out_proj), (scaled,) + row(width), (square,) + stat_row],
        [out((rows, width), f32, row(width)), out((8, rows), f32, stat_row)],
    )
    stats = small_sum(stats, "head")
    normal_gated, grad_ssd, grad_gate_in, row_term, state_grads, gate_sums, packed_back = call(
        partial(gate_kernel, float(width * ranks)),
        grid,
        [
            (ssd_out,) + row(width),
            (gate_in,) + row(width),
            (grad_normal,) + row(width),
            (stats, (8, BLOCK), lambda i, j: (0, i * blocks + j)),
            fixed(gain),
            fixed(skip),
            (x,) + row(width),
            (c,) + row(STATE),
            (cum,) + row(heads),
        ],
        [
            out((rows, width), bf16, row(width)),
            out((rows, width), bf16, row(width)),
            out((rows, width), bf16, row(width)),
            out((rows, heads), f32, row(heads)),
            out((count, STATE, width), f32, per_block(STATE, width)),
            ((8, width), f32, (8, width), lambda i, j: (0, 0)),
            out((batch, STATE + PAD, width), f32, per_batch(STATE + PAD, width)),
        ],
        [((STATE, width), f32), ((1, width), f32)],
    )
    leaving = carried_in(packed_back, "seq", True)
    grad_x_in, grad_b_in, grad_c_in = call(
        score_kernel,
        grid,
        [
            (x,) + row(width),
            (b,) + row(STATE),
            (c,) + row(STATE),
            (cum,) + row(heads),
            (cumt,) + per_block(heads, BLOCK),
            (step,) + row(heads),
            (grad_ssd,) + row(width),
        ],
        [
            out((rows, width), f32, row(width)),
            out((rows, STATE), f32, row(STATE)),
            out((rows, STATE), f32, row(STATE)),
        ],
        [((BLOCK, BLOCK), f32)],
    )

    def chunked(kernel, ins, more=()):
        return call(
            partial(kernel, ranks),
            grid,
            ins,
            [out((ranks, rows, part), bf16, ((ranks, BLOCK, part), lambda i, j: (0, i * blocks + j, 0)))] + list(more),
        )

    def scattered(result):
        index = lax.axis_index("head")
        route = [(i, (i + 1) % ranks) for i in range(ranks)]

        def own(back):
            return lax.dynamic_index_in_dim(result, (index - back) % ranks, 0, keepdims=False)

        total = own(1)
        for step in range(1, ranks):
            total = lax.ppermute(total, "head", route)
            total = total.astype(f32) + own(step + 1).astype(f32)
            if step < ranks - 1:
                total = total.astype(bf16)
        return total.reshape(batch, tokens, part)

    out_part = scattered(chunked(result_kernel, [(normal_gated,) + row(width), fixed(out_proj)])[0])
    block_out = (hidden.astype(f32) + out_part).astype(bf16)

    gate_proj_part = outer(normed, grad_gate_in, features, 6)
    out_proj_part = outer(normal_gated, cot_rows, width, 3)
    gate_proj_part, out_proj_part = lax.optimization_barrier((gate_proj_part, out_proj_part))
    out_proj_grad, gate_proj_grad = lax.psum((out_proj_part, gate_proj_part), "seq")

    taps = jnp.concatenate([conv_value, conv_state], 1)
    mix = width + maps
    grad_conv, tail, returned, grad_raw, sum_conv, sum_h = call(
        back_kernel,
        grid,
        [
            (leaving,) + per_batch(STATE, width),
            (starts,) + back_block(STATE, width),
            (state_grads,) + back_block(STATE, width),
            (grad_x_in,) + back_row(width),
            (grad_b_in,) + back_row(STATE),
            (grad_c_in,) + back_row(STATE),
            (row_term,) + back_row(heads),
            (x,) + back_row(width),
            (grad_ssd,) + back_row(width),
            (b,) + back_row(STATE),
            (c,) + back_row(STATE),
            (raw,) + back_row(heads),
            (step,) + back_row(heads),
            (cum,) + back_row(heads),
            (mixed,) + back_row(mix),
            (conv_in,) + back_row(mix),
            (conv_edge,) + per_batch(EDGE, mix),
            fixed(taps),
            fixed(skip),
            fixed(bias),
            fixed(rate),
        ],
        [
            out((rows, mix), bf16, back_row(mix)),
            out((batch, PAD, mix), f32, per_batch(PAD, mix)),
            out((batch, EDGE, mix), f32, per_batch(EDGE, mix)),
            out((rows, heads), bf16, back_row(heads)),
            ((8, mix), f32, (8, mix), lambda i, j: (0, 0)),
            ((8, heads), f32, (8, heads), lambda i, j: (0, 0)),
        ],
        [
            ((STATE, width), f32),
            ((BLOCK + EDGE, mix), f32),
            ((2 * EDGE, mix), f32),
        ],
    )
    given = passed_along(returned, "seq", -1)
    tail = jnp.concatenate([tail[:, : PAD - EDGE], tail[:, PAD - EDGE :] + given], 1).astype(bf16)
    grad_conv = lax.dynamic_update_slice(
        grad_conv.reshape(batch, tokens, mix), tail, (0, tokens - PAD, 0)
    ).reshape(rows, mix)

    half = features // 2
    seq_index, seq_size = lax.axis_index("seq"), lax.axis_size("seq")
    upper = seq_index % 2
    given_half = outer(normed, grad_conv, half, 3, 1 - upper, maps)
    given_half = lax.optimization_barrier((given_half, grad_conv))
    kept_half = outer(normed, given_half[1], half, 3, upper, maps)
    other_half = sent(given_half[0], "seq", 1)
    kept_half, conv_later, raw_later, gate_later = lax.optimization_barrier(
        (kept_half, grad_conv, grad_raw, grad_gate_in)
    )
    grad_chunks, norm_sums = chunked(
        chunk_kernel,
        [
            (gate_later,) + row(width),
            (conv_later,) + row(mix),
            (raw_later,) + row(heads),
            (normed,) + row(features),
            (inv_rms,) + row(128),
            fixed(lead(norm_gain)),
            fixed(gate_proj),
            fixed(value_proj),
            fixed(state_proj),
            fixed(step_proj),
        ],
        [((8, features), f32, (8, features), lambda i, j: (0, 0))],
    )
    grad_part = scattered(grad_chunks)
    planes = seq_size // 2
    plane = seq_index // 2
    lines = half // planes
    (_, kept_half) = lax.optimization_barrier((grad_chunks, kept_half))

    def line(value, at):
        return lax.dynamic_slice_in_dim(value, at * lines, lines, 0).astype(f32)

    value_quarters, maps_quarters = [], []
    for k in range(planes):
        total = line(kept_half, plane ^ k) + line(other_half, plane ^ k)
        value_quarters.append(total[:, :width].astype(bf16))
        maps_quarters.append((total[:, width:mix] + total[:, mix:]).astype(bf16))
    value_quarters, maps_quarters, grad_raw = lax.optimization_barrier((value_quarters, maps_quarters, grad_raw))

    def plane_sum(quarters):
        others = [sent(quarters[k], "seq", 2 * k) for k in range(1, planes)]
        return sum((other.astype(f32) for other in others), quarters[0].astype(f32)).astype(bf16)

    maps_part = plane_sum(maps_quarters)
    value = plane_sum(value_quarters)
    step_part = dot(grad_raw, normed, TN)

    def flat(block, lines):
        return jnp.pad(block.reshape(-1), (0, lines * features - block.size)).reshape(lines, features)

    folded = features // maps
    state_sums = jnp.pad(sum_conv[: CONV + 1, width:], ((0, 7 - CONV), (0, 0)))
    state_high = lax.reduce_precision(state_sums, 8, 7)
    norm_lines = jnp.pad(norm_sums[0].reshape(folded, maps), ((0, PAD - folded), (0, 0)))
    shared = jnp.concatenate([state_high, state_sums - state_high, norm_lines]).astype(bf16)
    shared = jnp.concatenate([maps_part, shared])
    shared = small_sum(shared, "head")
    maps_part, shared = shared[:lines].astype(bf16), shared[lines:]
    shared = jnp.concatenate([shared[:8] + shared[8:PAD], shared[PAD : PAD + 8]])
    small = jnp.concatenate(
        [
            jnp.pad(step_part, ((0, PAD - heads), (0, 0))),
            flat(jnp.concatenate([sum_conv[: CONV + 1, :width], gate_sums[:2]]), 4),
            flat(sum_h[:2], 1),
            flat(shared, 3),
        ]
    )
    out_proj_grad, gate_proj_grad = out_proj_grad.astype(f32), gate_proj_grad.astype(f32)
    mask = 1
    while mask < seq_size:
        other = sent(small, "seq", mask)
        small = small + other
        mask *= 2

    def rebuilt(quarter):
        pieces = [quarter] + [sent(quarter, "seq", 2 * k) for k in range(1, planes)]
        return ordered(pieces, plane ^ jnp.arange(planes))

    gathered = lax.all_gather(value, "seq")
    gathered = gathered.reshape(planes, 2, lines, width).swapaxes(0, 1).reshape(features, width)
    value_proj_grad = gathered.astype(f32)
    own_maps = rebuilt(maps_part)
    (state_proj_grad,) = joined(own_maps, sent(own_maps, "seq", 1), upper, (maps,))
    hidden_grad = (cotangent.astype(f32) + grad_part).astype(bf16)
    lined = small[PAD : PAD + 4].reshape(-1)[: (CONV + 3) * width].reshape(CONV + 3, width)
    sum_v, gate_sums = lined[: CONV + 1], lined[CONV + 1 :]
    sum_h = small[PAD + 4, : 2 * heads].reshape(2, heads)
    shared = small[PAD + 5 : PAD + 8].reshape(-1)[: PAD * maps].reshape(PAD, maps)
    sum_s, norm_gain_grad = shared[: CONV + 1], shared[8 : 8 + folded].reshape(features)
    return (
        block_out,
        hidden_grad,
        lax.dynamic_slice_in_dim(norm_gain_grad, head_index * part, part),
        gate_proj_grad,
        value_proj_grad,
        state_proj_grad,
        small[:heads].T,
        sum_v[:CONV],
        sum_v[CONV],
        sum_s[:CONV],
        sum_s[CONV],
        sum_h[0],
        sum_h[1],
        jnp.sum(gate_sums[1].reshape(heads, HEAD_DIM), -1),
        gate_sums[0],
        out_proj_grad,
    )


def solution(mesh):
    placed = (
        P(None, "seq", "head"),
        P(),
        P(None, "head"),
        P(None, "head"),
        P(),
        P(None, "head"),
        P(None, "head"),
        P("head"),
        P(),
        P(),
        P("head"),
        P("head"),
        P("head"),
        P("head"),
        P("head", None),
        P(None, "seq", "head"),
    )
    return jax.shard_map(
        body,
        mesh=mesh,
        in_specs=placed,
        out_specs=(
            P(None, "seq", "head"),
            P(None, "seq", "head"),
            P("head"),
            P(None, "head"),
            P(None, "head"),
            P(),
            P(None, "head"),
            P(None, "head"),
            P("head"),
            P(),
            P(),
            P("head"),
            P("head"),
            P("head"),
            P("head"),
            P("head", None),
        ),
        check_vma=False,
    )
```
